32 devices in a mesh: grp: 4 (over z), tile: 2 (over y), arch: 4 (over x, core).
Axes of the slice: x: 2, y: 2, z: 4, core: 2. Of those that a mesh axis runs over, the one named last changes fastest.
Arguments:
- query_grads: bfloat16 [4, 1536, 4096], P('arch', 'tile', 'grp'), may hold values from -6 to 6
- input_basis: bfloat16 [4096, 4096], P(None, 'grp'), may hold values from -0.09375 to 0.09375
- output_basis: bfloat16 [1536, 1536], P(None, 'tile'), may hold values from -0.15625 to 0.15625
- eigenvalues: float32 [1536, 4096], P('tile', 'grp'), may hold values from 0.1 to 10
- activations: bfloat16 [1024, 4096], P('arch', 'grp'), may hold values from -6 to 6
- gradients: bfloat16 [1024, 1536], P('arch', 'tile'), may hold values from -0.0099487305 to 0.0099487305
- seq_lengths: int32 [4, 8], P('arch'), may hold values from 1 to 128, 256 in all within a row
Outputs:
- preconditioned: bfloat16 [4, 4096, 1536], P('arch', 'grp', 'tile')
- sequence_scores: float32 [4, 32], P(None, 'arch')
The draws below stay inside these ranges and needn't reach their ends.
Inputs may be any that keep to these rules, and one draw needn't show every extreme that they name: Each row of seq_lengths sums to 256, and its largest entry is exactly 128.
All inputs are finite; a program needn't handle non-finite values.
Results may differ from the reference program's by a relative error of at most 0.013.
Values may be sent and summed in bfloat16 or wider, within the bound.
No kernel may reach another device: no remote copies, remote signals or barrier semaphores. Data moves between devices by JAX's collectives and lax.ppermute only.
A program may use at most 64 MiB of HBM per device.

```python
import math
import jax
import jax.numpy as jnp
import numpy as np
from jax import lax

D = 4096
F = 1536
NQ = 4
ROWS_DEV = 256
SEQS_DEV = 8
ROWS = 1024
MOST = 128
N_TILE = 2
N_ARCH = 4


def block_scale(key, extent, shards, least, high):
    level = 1.0
    for dim, shards_of in shards:
        steps = jax.random.uniform(jax.random.fold_in(jax.random.fold_in(key, 6), dim), (shards_of,), jnp.float32, least / len(shards), high / len(shards))
        level = level * jnp.repeat(jnp.exp(steps), extent[dim] // shards_of).reshape((-1,) + (1,) * (len(extent) - 1 - dim))
    return level


def profile(count, total, most, lean):
    portions = [(1 << 20) // math.isqrt(rank ** lean) + 1 for rank in range(2, count + 1)]
    spare, given = total - most - (count - 1), [1] * (count - 1)
    while spare > 0:
        free = [i for i in range(count - 1) if given[i] < most]
        whole, remaining = sum([portions[i] for i in free]), spare
        for i in free:
            more = min(most - given[i], max(1, remaining * portions[i] // whole), spare)
            given[i] = given[i] + more
            spare = spare - more
    return np.array([most] + given)


def uneven(own_key, amount, total, bound, skew):
    if amount == 2:
        one = jax.random.randint(own_key, (), max(1, total - bound), min(bound, total - 1) + 1)
        return jnp.stack([one, total - one])
    lengths = jnp.asarray(profile(amount, total, bound, skew), jnp.int32)
    couples = (amount - 1) // 2
    donor, taker = lengths[1:1 + 2 * couples:2], lengths[2:2 + 2 * couples:2]
    slack = jnp.minimum(donor - 1, bound - taker)
    passed = jax.random.randint(jax.random.fold_in(own_key, 1), (couples,), 0, 1 << 20) % (slack + 1)
    lengths = lengths.at[1:1 + 2 * couples:2].set(donor - passed).at[2:2 + 2 * couples:2].set(taker + passed)
    return lengths[jax.random.permutation(jax.random.fold_in(own_key, 2), amount)]


def bell_draw(rng, extent, deviation, limit, shards=(), held_as=jnp.bfloat16):
    values = deviation * jax.random.normal(rng, extent, jnp.float32)
    if shards:
        values = values * block_scale(rng, extent, shards, -0.22, 0.18)
    return jnp.clip(values, -limit, limit).astype(held_as)


def setup_inputs(seed: int = 0) -> dict:
    keys = jax.random.split(jax.random.key(seed), 8)
    return {
        "query_grads": bell_draw(keys[0], (NQ, F, D), 1.0, 6.0, ((0, 4), (1, 2), (2, 4))),
        "input_basis": bell_draw(keys[1], (D, D), D ** -0.5, 0.09375, ((1, 4),)),
        "output_basis": bell_draw(keys[2], (F, F), F ** -0.5, 0.15625, ((1, 2),)),
        "eigenvalues": jnp.clip(jnp.exp(math.log(10.0) - 4.6051702 * jax.random.uniform(keys[3], (F, D), jnp.float32) ** block_scale(keys[3], (F, D), ((0, 2), (1, 4)), -0.2, 0.2)), 0.1, 10.0),
        "activations": bell_draw(keys[4], (ROWS, D), 1.0, 6.0, ((0, 4), (1, 4))),
        "gradients": bell_draw(keys[5], (ROWS, F), 0.0015, 0.0099487305, ((0, 4), (1, 2))),
        "seq_lengths": jax.vmap(lambda own: uneven(own, SEQS_DEV, ROWS_DEV, MOST, 1))(jax.random.split(keys[6], N_ARCH)).reshape((N_ARCH, SEQS_DEV)).astype(jnp.int32),
    }


damping = 0.01


def reference(query_grads, input_basis, output_basis, eigenvalues, activations, gradients, seq_lengths):
    block = F // N_TILE
    grads_f = gradients.astype(jnp.float32)
    pre_list = []
    score_list = []
    for query in range(NQ):
        rotated_in = jnp.dot(query_grads[query], input_basis, preferred_element_type=jnp.float32).astype(jnp.bfloat16)
        rotated = jnp.dot(output_basis.T, rotated_in, preferred_element_type=jnp.float32)
        scaled = (rotated / (eigenvalues + damping)).astype(jnp.bfloat16)
        restored = jnp.zeros((F, D), jnp.float32)
        for index in range(N_TILE):
            product = jnp.dot(output_basis[:, index * block:(index + 1) * block], scaled[index * block:(index + 1) * block, :], preferred_element_type=jnp.float32)
            restored = restored + lax.optimization_barrier(product.astype(jnp.bfloat16)).astype(jnp.float32)
        restored = restored.astype(jnp.bfloat16)
        precond = jnp.dot(input_basis, restored.T, preferred_element_type=jnp.float32).astype(jnp.bfloat16)
        pre_list.append(precond)
        projected = jnp.dot(activations, precond, preferred_element_type=jnp.float32)
        score_list.append(jnp.sum(projected * grads_f, axis=1))
    preconditioned = jnp.stack(pre_list, axis=0)
    token_scores = jnp.stack(score_list, axis=0).reshape(NQ, N_ARCH, ROWS_DEV)
    ends = jnp.cumsum(seq_lengths, axis=1)
    starts = ends - seq_lengths
    position = jnp.arange(ROWS_DEV, dtype=jnp.int32)
    member = ((position[None, None, :] >= starts[:, :, None]) & (position[None, None, :] < ends[:, :, None])).astype(jnp.float32)
    totals = jnp.einsum("qar,asr->qas", token_scores, member, precision=lax.Precision.HIGHEST)
    sequence_scores = (totals / seq_lengths.astype(jnp.float32)[None, :, :]).reshape(NQ, N_ARCH * SEQS_DEV)
    return preconditioned, sequence_scores
```

```python
import jax
import jax.numpy as jnp
from jax import lax
from jax.sharding import PartitionSpec as P

damping = 0.01
f32 = jnp.float32
bf16 = jnp.bfloat16


def mm(a, b):
    return lax.dot_general(a, b, (((1,), (0,)), ((), ())), preferred_element_type=f32)


def mm_tn(a, b):
    return lax.dot_general(a, b, (((0,), (0,)), ((), ())), preferred_element_type=f32)


def mm_nt(a, b):
    return lax.dot_general(a, b, (((1,), (1,)), ((), ())), preferred_element_type=f32)


def folded(n):
    return [0] + list(range(1, n, 2)) + [i for i in range(n - 1, 0, -1) if i % 2 == 0]


def shift(x, axis, n, k):
    return lax.ppermute(x, axis, [(i, (i + k) % n) for i in range(n)])


def rows_at(x, start, size):
    return lax.dynamic_slice_in_dim(x, start, size, 0)


def cols_at(x, start, size):
    return lax.dynamic_slice_in_dim(x, start, size, 1)


def make(n_grp, n_tile, n_arch):
    ring = folded(n_grp)
    fw = [(ring[i], ring[(i + 1) % n_grp]) for i in range(n_grp)]
    bw = [(b, a) for a, b in fw]
    place = [ring.index(i) for i in range(n_grp)]

    def per_device(query_grads, input_basis, output_basis, eigenvalues, activations, gradients, seq_lengths):
        query = query_grads[0]
        nf, nd = query.shape
        width = nd // n_tile
        rows = activations.shape[0]
        grp, tile = lax.axis_index("grp"), lax.axis_index("tile")
        order = jnp.asarray(ring, jnp.int32)
        pos = jnp.asarray(place, jnp.int32)[grp]

        def at(k):
            return order[(pos + k) % n_grp]

        half = nf // 2
        top, low = query[:half], query[half:]
        own_rows = rows_at(input_basis, grp * nd, nd)
        acc_top, acc_low = mm(top, own_rows), mm(low, own_rows)
        for s in range(1, n_grp):
            top = lax.ppermute(top, "grp", fw)
            low = lax.ppermute(low, "grp", bw)
            acc_top += mm(top, rows_at(input_basis, at(-s) * nd, nd))
            acc_low += mm(low, rows_at(input_basis, at(s) * nd, nd))
        rotated_in = jnp.concatenate([acc_top.astype(bf16), acc_low.astype(bf16)], axis=0)

        bases, values = [output_basis], []
        for k in range(1, n_tile):
            bases.append(shift(output_basis, "tile", n_tile, k))
        values.append(cols_at(eigenvalues, tile * width, width))
        for k in range(1, n_tile):
            sent = cols_at(eigenvalues, ((tile + k) % n_tile) * width, width)
            values.append(shift(sent, "tile", n_tile, k))
        all_acts, all_grads = [activations], [gradients]
        for k in range(1, n_arch):
            all_acts.append(shift(activations, "arch", n_arch, k))
            all_grads.append(shift(gradients, "arch", n_arch, k))
        all_acts = jnp.concatenate(all_acts, axis=0)
        all_grads = jnp.concatenate(all_grads, axis=0)

        parts = [cols_at(rotated_in, tile * width, width)]
        for k in range(1, n_tile):
            sent = cols_at(rotated_in, ((tile + k) % n_tile) * width, width)
            parts.append(shift(sent, "tile", n_tile, k))
        scaled = []
        for basis, value in zip(bases, values):
            rotated = 0.0
            for k, part in enumerate(parts):
                rotated += mm_tn(rows_at(basis, ((tile - k) % n_tile) * nf, nf), part)
            scaled.append((rotated / (value + damping)).astype(bf16))
        back = []
        for k in range(n_tile):
            restored = 0.0
            for basis, one in zip(bases, scaled):
                restored += mm(rows_at(basis, ((tile + k) % n_tile) * nf, nf), one)
            restored = restored.astype(bf16)
            back.append(shift(restored, "tile", n_tile, k) if k else restored)
        restored = jnp.zeros((nf, nd), bf16)
        for k, one in enumerate(back):
            restored = lax.dynamic_update_slice_in_dim(restored, one, ((tile - k) % n_tile) * width, 1)

        hd = nd // 2

        def share(owner, low_half):
            return mm_nt(rows_at(input_basis, owner * nd + (hd if low_half else 0), hd), restored)

        top = share(at(-1), False).astype(bf16)
        low = share(at(1), True).astype(bf16)
        for s in range(2, n_grp + 1):
            top = lax.ppermute(top, "grp", fw)
            low = lax.ppermute(low, "grp", bw)
            top = (share(at(-s), False) + top.astype(f32)).astype(bf16)
            low = (share(at(s), True) + low.astype(f32)).astype(bf16)
        preconditioned = jnp.concatenate([top, low], axis=0)

        projected = mm(all_acts, preconditioned)
        tokens = jnp.sum(projected * all_grads.astype(f32), axis=1).reshape(n_arch, rows)
        token_parts = [tokens[0]]
        for k in range(1, n_arch):
            token_parts.append(shift(tokens[k], "arch", n_arch, n_arch - k))
        lengths = seq_lengths[0]
        ends = jnp.cumsum(lengths)
        starts = ends - lengths
        position = jnp.arange(rows, dtype=jnp.int32)
        member = ((position[None, :] >= starts[:, None]) & (position[None, :] < ends[:, None])).astype(f32)
        by_query = jnp.stack(token_parts, axis=0)
        by_query = jnp.roll(by_query, lax.axis_index("arch"), axis=0)
        totals = jnp.dot(by_query, member.T, precision=lax.Precision.HIGHEST)
        for axis, n in (("tile", n_tile), ("grp", n_grp)):
            totals = sum([shift(totals, axis, n, k) for k in range(1, n)], totals)
        return preconditioned[None], totals / lengths.astype(f32)[None, :]

    return per_device


def solution(mesh):
    n_grp, n_tile, n_arch = mesh.shape["grp"], mesh.shape["tile"], mesh.shape["arch"]
    return jax.shard_map(
        make(n_grp, n_tile, n_arch),
        mesh=mesh,
        in_specs=(
            P("arch", "tile", "grp"),
            P(None, "grp"),
            P(None, "tile"),
            P("tile", "grp"),
            P("arch", "grp"),
            P("arch", "tile"),
            P("arch", None),
        ),
        out_specs=(P("arch", "grp", "tile"), P(None, "arch")),
        check_vma=False,
    )
```

```python
import jax
import jax.numpy as jnp
from jax import lax
from jax.experimental import pallas as pl
from jax.experimental.pallas import tpu as pltpu
from jax.sharding import PartitionSpec as P

damping = 0.01
f32 = jnp.float32
bf16 = jnp.bfloat16


def mm(a, b):
    return lax.dot_general(a, b, (((1,), (0,)), ((), ())), preferred_element_type=f32)


def mm_tn(a, b):
    return lax.dot_general(a, b, (((0,), (0,)), ((), ())), preferred_element_type=f32)


def mm_tt(a, b):
    return lax.dot_general(a, b, (((0,), (1,)), ((), ())), preferred_element_type=f32)


def folded(n):
    return [0] + list(range(1, n, 2)) + [i for i in range(n - 1, 0, -1) if i % 2 == 0]


def rows_at(x, start, size):
    return lax.dynamic_slice_in_dim(x, start, size, 0)


def cols_at(x, start, size):
    return lax.dynamic_slice_in_dim(x, start, size, 1)


def assemble(where_to, local, pieces):
    size = pieces[0].shape[0]
    count = len(pieces)

    def kernel(where_ref, local_ref, *refs):
        out_ref, held, read, written = refs[count:]
        starts = [pl.multiple_of(where_ref[i + 1], size) for i in range(count)]

        def inward(i, of_local):
            source = local_ref.at[pl.ds(starts[i], size)] if of_local else refs[i]
            return pltpu.make_async_copy(source, held.at[i], read.at[i])

        def outward(i):
            return pltpu.make_async_copy(held.at[i], out_ref.at[pl.ds(starts[i], size)], written.at[i])

        for of_local in (True, False):

            @pl.when(where_ref[0] == (1 if of_local else 0))
            def _():
                for i in range(count):
                    inward(i, of_local).start()
                for i in range(count):
                    inward(i, of_local).wait()
                    outward(i).start()

        for i in range(count):
            outward(i).wait()

    return pl.pallas_call(
        kernel,
        out_shape=jax.ShapeDtypeStruct(local.shape, local.dtype),
        in_specs=[pl.BlockSpec(memory_space=pltpu.SMEM)] + [pl.BlockSpec(memory_space=pl.ANY)] * (count + 1),
        out_specs=pl.BlockSpec(memory_space=pl.ANY),
        scratch_shapes=[
            pltpu.VMEM((count,) + pieces[0].shape, local.dtype),
            pltpu.SemaphoreType.DMA((count,)),
            pltpu.SemaphoreType.DMA((count,)),
        ],
        name="assemble",
    )(where_to, local, *pieces)


def make(n_grp, n_tile, n_arch):
    n_half, n_x = n_grp // 2, n_arch // 2
    ring = folded(n_half)

    def half_of(g):
        return g // n_half

    def far(g):
        return (g + n_half) % n_grp

    def home(g, a):
        return a % 2 == half_of(g)

    def number(g, t, a):
        return (g * n_tile + t) * n_arch + a

    def send(x, to):
        pairs = []
        for g in range(n_grp):
            for t in range(n_tile):
                for a in range(n_arch):
                    other = to(g, t, a)
                    if other is not None:
                        pairs.append((number(g, t, a), number(*other)))
        return lax.ppermute(x, ("grp", "tile", "arch"), pairs)

    def cross(x):
        return send(x, lambda g, t, a: None if home(g, a) else (far(g), t, a ^ 1))

    def core(x):
        return send(x, lambda g, t, a: (g, t, a ^ 1))

    def onward(x, only=None):
        def to(g, t, a):
            if only is not None and home(g, a) != only:
                return None
            after = ring[(ring.index(g % n_half) + 1) % n_half]
            return (half_of(g) * n_half + after, t, a)

        return send(x, to)

    def to_tile(x, k, only=None):
        return send(x, lambda g, t, a: (g, (t + k) % n_tile, a) if only is None or home(g, a) == only else None)

    def to_x(x, k):
        return send(x, lambda g, t, a: None if home(g, a) else (g, t, (a + 2 * k) % n_arch))

    def to_arch(x, k):
        return send(x, lambda g, t, a: (g, t, (a + k) % n_arch))

    def to_grp(x, k):
        return send(x, lambda g, t, a: ((g + k) % n_grp, t, a))

    def to_away(x):
        return send(x, lambda g, t, a: (far(g), t, a) if home(g, a) else None)

    def per_device(query_grads, input_basis, output_basis, eigenvalues, activations, gradients, seq_lengths):
        query = query_grads[0]
        nf, nd = query.shape
        width = nd // n_tile
        rows = activations.shape[0]
        grp, tile, arch = lax.axis_index("grp"), lax.axis_index("tile"), lax.axis_index("arch")
        mine = arch % 2
        plane_half = grp // n_half
        at_home = mine == plane_half
        order = jnp.asarray(ring, jnp.int32)
        pos = jnp.asarray([ring.index(i) for i in range(n_half)], jnp.int32)[grp % n_half]
        own_base = mine * n_half
        other_base = n_half - own_base

        def at(k):
            return order[(pos + k) % n_half]

        parts = n_tile * n_x
        part = input_basis.shape[0] // parts
        piece = part // 2
        place_t, place_x = tile, arch // 2
        pieces = []
        for e in range(2):
            start = (place_t * n_x + place_x) * part + e * piece
            own = lax.optimization_barrier(rows_at(input_basis, start, piece))
            own = to_away(own)
            if e == 0:
                held = [(0, 0, own)]
                held += [(k, 0, to_tile(own, k, False)) for k in range(1, n_tile)]
                held += [(kt, k, to_x(one, k)) for k in range(1, n_x) for kt, _, one in list(held)]
            else:
                held = [(0, 0, own)]
                held += [(0, k, to_x(own, k)) for k in range(1, n_x)]
                held += [(k, kx, to_tile(one, k, False)) for k in range(1, n_tile) for _, kx, one in list(held)]
            pieces += [(kt, kx, e, one) for kt, kx, one in held]
        starts = [
            (((place_t - kt) % n_tile) * n_x + (place_x - kx) % n_x) * part + e * piece
            for kt, kx, e, _ in pieces
        ]
        where_to = jnp.stack([at_home.astype(jnp.int32)] + [one.astype(jnp.int32) for one in starts])
        basis = assemble(where_to, input_basis, [one for _, _, _, one in pieces])

        half = nf // 2
        sums = []
        for e in range(2):
            held = query[e * half : (e + 1) * half]
            held = jnp.where(at_home, held, cross(held))
            total = 0.0
            for s in range(n_half):
                if s:
                    held = onward(held)
                theirs = core(held)
                total += mm(held, rows_at(basis, (own_base + at(-s)) * nd, nd))
                total += mm(theirs, rows_at(basis, (other_base + at(-s)) * nd, nd))
            sums.append(total.astype(bf16))
        rotated_in = jnp.concatenate(sums, axis=0)

        bases = [output_basis]
        hv = output_basis.shape[0] // 2
        for k in range(1, n_tile):
            one = to_tile(rows_at(output_basis, mine * hv, hv), k)
            two = core(one)
            whole = jnp.zeros_like(output_basis)
            whole = lax.dynamic_update_slice_in_dim(whole, one, mine * hv, 0)
            bases.append(lax.dynamic_update_slice_in_dim(whole, two, (1 - mine) * hv, 0))
        factor = (1.0 / (eigenvalues + damping)).astype(bf16)
        factors = [cols_at(factor, tile * width, width)]
        for k in range(1, n_tile):
            one = cols_at(factor, ((tile + k) % n_tile) * width, width)
            factors.append(to_tile(one, k, True))
        factors = jnp.concatenate(factors, axis=0)
        portion = factors.shape[0] // n_x
        place = arch // 2
        one = to_away(rows_at(factors, place * portion, portion))
        away = lax.dynamic_update_slice_in_dim(jnp.zeros_like(factors), one, place * portion, 0)
        for k in range(1, n_x):
            away = lax.dynamic_update_slice_in_dim(away, to_x(one, k), ((place - k) % n_x) * portion, 0)
        factors = jnp.where(at_home, factors, away)
        factors = [factors[k * nf : (k + 1) * nf] for k in range(n_tile)]
        both = jnp.concatenate([activations, gradients], axis=1)
        both = [both] + [to_arch(both, k) for k in range(1, n_arch)]
        both = jnp.concatenate(both, axis=0)

        parts = [cols_at(rotated_in, tile * width, width)]
        for k in range(1, n_tile):
            one = cols_at(rotated_in, ((tile + k) % n_tile) * width, width)
            parts.append(to_tile(one, k))
        scaled = []
        for one_basis, one_factor in zip(bases, factors):
            rotated = 0.0
            for k, one in enumerate(parts):
                rotated += mm_tn(rows_at(one_basis, ((tile - k) % n_tile) * nf, nf), one)
            scaled.append((rotated * one_factor.astype(f32)).astype(bf16))
        restored = jnp.zeros((nd, nf), bf16)
        for k in range(n_tile):
            back = 0.0
            for one_basis, one in zip(bases, scaled):
                back += mm_tt(one, rows_at(one_basis, ((tile + k) % n_tile) * nf, nf))
            back = back.astype(bf16)
            if k:
                back = to_tile(back, k)
            restored = lax.dynamic_update_slice_in_dim(restored, back, ((tile - k) % n_tile) * width, 0)

        hd = nd // 2

        def product(block, e):
            return mm(rows_at(basis, block * nd + e * hd, hd), restored)

        outs = []
        for e in range(2):
            for s in range(1, n_half + 1):
                theirs = product(other_base + at(-s), e).astype(bf16)
                theirs = core(theirs)
                added = product(own_base + at(-s), e) + theirs.astype(f32)
                if s > 1:
                    added = lax.optimization_barrier(added)
                    away_total = (added + onward(away_total, False).astype(f32)).astype(bf16)
                    home_total = (added + onward(home_total, True).astype(f32)).astype(bf16)
                else:
                    away_total = home_total = added.astype(bf16)
            outs.append(jnp.where(at_home, home_total, cross(away_total)))
        preconditioned = jnp.concatenate(outs, axis=0)
        all_acts, all_grads = both[:, :nd], both[:, nd:]

        projected = mm(all_acts, preconditioned)
        tokens = jnp.sum(projected * all_grads.astype(f32), axis=1).reshape(n_arch, rows)
        token_parts = [tokens[0]]
        for k in range(1, n_arch):
            token_parts.append(to_arch(tokens[k], n_arch - k))
        lengths = seq_lengths[0]
        ends = jnp.cumsum(lengths)
        starts = ends - lengths
        position = jnp.arange(rows, dtype=jnp.int32)
        member = ((position[None, :] >= starts[:, None]) & (position[None, :] < ends[:, None])).astype(f32)
        totals = [jnp.dot(one[None], member.T, precision=lax.Precision.HIGHEST) for one in token_parts]
        totals = jnp.concatenate(totals, axis=0)
        totals = sum([to_tile(totals, k) for k in range(1, n_tile)], totals)
        totals = sum([to_grp(totals, k) for k in range(1, n_grp)], totals)
        scores = totals / lengths.astype(f32)[None, :]
        return preconditioned[None], jnp.roll(scores, arch, axis=0)

    return per_device


def solution(mesh):
    n_grp, n_tile, n_arch = mesh.shape["grp"], mesh.shape["tile"], mesh.shape["arch"]
    return jax.shard_map(
        make(n_grp, n_tile, n_arch),
        mesh=mesh,
        in_specs=(
            P("arch", "tile", "grp"),
            P(None, "grp"),
            P(None, "tile"),
            P("tile", "grp"),
            P("arch", "grp"),
            P("arch", "tile"),
            P("arch", None),
        ),
        out_specs=(P("arch", "grp", "tile"), P(None, "arch")),
        check_vma=False,
    )
```

```python
import jax
import jax.numpy as jnp
from jax import lax
from jax.experimental import pallas as pl
from jax.experimental.pallas import tpu as pltpu
from jax.sharding import PartitionSpec as P

damping = 0.01
f32 = jnp.float32
bf16 = jnp.bfloat16


def mm(a, b):
    return lax.dot_general(a, b, (((1,), (0,)), ((), ())), preferred_element_type=f32)


def mm_tn(a, b):
    return lax.dot_general(a, b, (((0,), (0,)), ((), ())), preferred_element_type=f32)


def mm_tt(a, b):
    return lax.dot_general(a, b, (((0,), (1,)), ((), ())), preferred_element_type=f32)


def folded(n):
    return [0] + list(range(1, n, 2)) + [i for i in range(n - 1, 0, -1) if i % 2 == 0]


def rows_at(x, start, size):
    return lax.dynamic_slice_in_dim(x, start, size, 0)


def cols_at(x, start, size):
    return lax.dynamic_slice_in_dim(x, start, size, 1)


def assemble(where_to, local, pieces):
    size = pieces[0].shape[0]
    count = len(pieces)

    def kernel(where_ref, local_ref, *refs):
        out_ref, held, read, written = refs[count:]
        starts = [pl.multiple_of(where_ref[i + 1], size) for i in range(count)]

        def inward(i, of_local):
            source = local_ref.at[pl.ds(starts[i], size)] if of_local else refs[i]
            return pltpu.make_async_copy(source, held.at[i], read.at[i])

        def outward(i):
            return pltpu.make_async_copy(held.at[i], out_ref.at[pl.ds(starts[i], size)], written.at[i])

        for of_local in (True, False):

            @pl.when(where_ref[0] == (1 if of_local else 0))
            def _():
                for i in range(count):
                    inward(i, of_local).start()
                for i in range(count):
                    inward(i, of_local).wait()
                    outward(i).start()

        for i in range(count):
            outward(i).wait()

    return pl.pallas_call(
        kernel,
        out_shape=jax.ShapeDtypeStruct(local.shape, local.dtype),
        in_specs=[pl.BlockSpec(memory_space=pltpu.SMEM)] + [pl.BlockSpec(memory_space=pl.ANY)] * (count + 1),
        out_specs=pl.BlockSpec(memory_space=pl.ANY),
        scratch_shapes=[
            pltpu.VMEM((count,) + pieces[0].shape, local.dtype),
            pltpu.SemaphoreType.DMA((count,)),
            pltpu.SemaphoreType.DMA((count,)),
        ],
        name="as",
    )(where_to, local, *pieces)


def make(n_grp, n_tile, n_arch):
    n_half, n_x = n_grp // 2, n_arch // 2
    ring = folded(n_half)

    def half_of(g):
        return g // n_half

    def far(g):
        return (g + n_half) % n_grp

    def home(g, a):
        return a % 2 == half_of(g)

    def number(g, t, a):
        return (g * n_tile + t) * n_arch + a

    def send(x, to):
        pairs = []
        for g in range(n_grp):
            for t in range(n_tile):
                for a in range(n_arch):
                    other = to(g, t, a)
                    if other is not None:
                        pairs.append((number(g, t, a), number(*other)))
        return lax.ppermute(x, ("grp", "tile", "arch"), pairs)

    def cross(x):
        return send(x, lambda g, t, a: None if home(g, a) else (far(g), t, a ^ 1))

    def core(x):
        return send(x, lambda g, t, a: (g, t, a ^ 1))

    def onward(x, only=None):
        def to(g, t, a):
            if only is not None and home(g, a) != only:
                return None
            after = ring[(ring.index(g % n_half) + 1) % n_half]
            return (half_of(g) * n_half + after, t, a)

        return send(x, to)

    def to_tile(x, k, only=None):
        return send(x, lambda g, t, a: (g, (t + k) % n_tile, a) if only is None or home(g, a) == only else None)

    def to_x(x, k):
        return send(x, lambda g, t, a: None if home(g, a) else (g, t, (a + 2 * k) % n_arch))

    def to_arch(x, k):
        return send(x, lambda g, t, a: (g, t, (a + k) % n_arch))

    def to_grp(x, k):
        return send(x, lambda g, t, a: ((g + k) % n_grp, t, a))

    def to_away(x):
        return send(x, lambda g, t, a: (far(g), t, a) if home(g, a) else None)

    def per_device(query_grads, input_basis, output_basis, eigenvalues, activations, gradients, seq_lengths):
        query = query_grads[0]
        nf, nd = query.shape
        width = nd // n_tile
        rows = activations.shape[0]
        grp, tile, arch = lax.axis_index("grp"), lax.axis_index("tile"), lax.axis_index("arch")
        mine = arch % 2
        plane_half = grp // n_half
        at_home = mine == plane_half
        order = jnp.asarray(ring, jnp.int32)
        pos = jnp.asarray([ring.index(i) for i in range(n_half)], jnp.int32)[grp % n_half]
        own_base = mine * n_half
        other_base = n_half - own_base

        def at(k):
            return order[(pos + k) % n_half]

        parts = n_tile * n_x
        part = input_basis.shape[0] // parts
        piece = part // 2
        place_t, place_x = tile, arch // 2
        pieces = []
        for e in range(2):
            start = (place_t * n_x + place_x) * part + e * piece
            own = lax.optimization_barrier(rows_at(input_basis, start, piece))
            own = to_away(own)
            if e == 0:
                held = [(0, 0, own)]
                held += [(k, 0, to_tile(own, k, False)) for k in range(1, n_tile)]
                held += [(kt, k, to_x(one, k)) for k in range(1, n_x) for kt, _, one in list(held)]
            else:
                held = [(0, 0, own)]
                held += [(0, k, to_x(own, k)) for k in range(1, n_x)]
                held += [(k, kx, to_tile(one, k, False)) for k in range(1, n_tile) for _, kx, one in list(held)]
            pieces += [(kt, kx, e, one) for kt, kx, one in held]
        starts = [
            (((place_t - kt) % n_tile) * n_x + (place_x - kx) % n_x) * part + e * piece
            for kt, kx, e, _ in pieces
        ]
        where_to = jnp.stack([at_home.astype(jnp.int32)] + [one.astype(jnp.int32) for one in starts])
        basis = assemble(where_to, input_basis, [one for _, _, _, one in pieces])

        half = nf // 2
        sums = []
        for e in range(2):
            held = query[e * half : (e + 1) * half]
            held = jnp.where(at_home, held, cross(held))
            total = 0.0
            for s in range(n_half):
                if s:
                    held = onward(held)
                theirs = core(held)
                total += mm(held, rows_at(basis, (own_base + at(-s)) * nd, nd))
                total += mm(theirs, rows_at(basis, (other_base + at(-s)) * nd, nd))
            sums.append(total.astype(bf16))
        rotated_in = jnp.concatenate(sums, axis=0)

        bases = [output_basis]
        hv = output_basis.shape[0] // 2
        for k in range(1, n_tile):
            one = to_tile(rows_at(output_basis, mine * hv, hv), k)
            two = core(one)
            whole = jnp.zeros_like(output_basis)
            whole = lax.dynamic_update_slice_in_dim(whole, one, mine * hv, 0)
            bases.append(lax.dynamic_update_slice_in_dim(whole, two, (1 - mine) * hv, 0))
        factor = (1.0 / (eigenvalues + damping)).astype(bf16)
        factors = [cols_at(factor, tile * width, width)]
        for k in range(1, n_tile):
            one = cols_at(factor, ((tile + k) % n_tile) * width, width)
            factors.append(to_tile(one, k, True))
        factors = jnp.concatenate(factors, axis=0)
        portion = factors.shape[0] // n_x
        place = arch // 2
        one = to_away(rows_at(factors, place * portion, portion))
        away = lax.dynamic_update_slice_in_dim(jnp.zeros_like(factors), one, place * portion, 0)
        for k in range(1, n_x):
            other = to_x(one, k)
            away = lax.dynamic_update_slice_in_dim(away, other, ((place - k) % n_x) * portion, 0)
        factors = jnp.where(at_home, factors, away)
        factors = [factors[k * nf : (k + 1) * nf] for k in range(n_tile)]
        both = jnp.concatenate([activations, gradients], axis=1)
        both = [both] + [to_arch(both, k) for k in range(1, n_arch)]
        both = jnp.concatenate(both, axis=0)

        restored = jnp.zeros((nd, nf), bf16)
        chunk = width // 2
        for c in range(width // chunk):
            parts = []
            for k in range(n_tile):
                one = cols_at(rotated_in, ((tile + k) % n_tile) * width + c * chunk, chunk)
                parts.append(to_tile(one, k) if k else one)
            scaled = []
            for one_basis, one_factor in zip(bases, factors):
                rotated = 0.0
                for k, one in enumerate(parts):
                    rotated += mm_tn(rows_at(one_basis, ((tile - k) % n_tile) * nf, nf), one)
                one_factor = one_factor[:, c * chunk : (c + 1) * chunk]
                scaled.append((rotated * one_factor.astype(f32)).astype(bf16))
            for k in reversed(range(n_tile)):
                back = 0.0
                for one_basis, one in zip(bases, scaled):
                    back += mm_tt(one, rows_at(one_basis, ((tile + k) % n_tile) * nf, nf))
                back = back.astype(bf16)
                if k:
                    back = to_tile(back, k)
                restored = lax.dynamic_update_slice_in_dim(
                    restored, back, ((tile - k) % n_tile) * width + c * chunk, 0
                )

        hd = nd // 2

        def product(block, e):
            return mm(rows_at(basis, block * nd + e * hd, hd), restored)

        outs = []
        for e in range(2):
            added = []
            for s in range(1, n_half + 1):
                theirs = product(other_base + at(-s), e).astype(bf16)
                theirs = core(theirs)
                one = product(own_base + at(-s), e) + theirs.astype(f32)
                added.append(one.astype(bf16) if s == 1 else lax.optimization_barrier(one))
            away_total = added[0]
            for one in added[1:]:
                away_total = (one + onward(away_total, False).astype(f32)).astype(bf16)
            if e == 0:
                tick = send(away_total[:16, :128], lambda g, t, a: None if home(g, a) else (g, t, a ^ 1))
            home_total, _ = lax.optimization_barrier((added[0], tick))
            for one in added[1:]:
                home_total = (one + onward(home_total, True).astype(f32)).astype(bf16)
            outs.append(jnp.where(at_home, home_total, cross(away_total)))
        preconditioned = jnp.concatenate(outs, axis=0)
        all_acts, all_grads = both[:, :nd], both[:, nd:]

        projected = mm(all_acts, preconditioned)
        tokens = jnp.sum(projected * all_grads.astype(f32), axis=1).reshape(n_arch, rows)
        token_parts = [tokens[0]]
        for k in range(1, n_arch):
            token_parts.append(to_arch(tokens[k], n_arch - k))
        lengths = seq_lengths[0]
        ends = jnp.cumsum(lengths)
        starts = ends - lengths
        position = jnp.arange(rows, dtype=jnp.int32)
        member = ((position[None, :] >= starts[:, None]) & (position[None, :] < ends[:, None])).astype(f32)
        totals = [jnp.dot(one[None], member.T, precision=lax.Precision.HIGHEST) for one in token_parts]
        totals = jnp.concatenate(totals, axis=0)
        totals = sum([to_tile(totals, k) for k in range(1, n_tile)], totals)
        totals = sum([to_grp(totals, k) for k in range(1, n_grp)], totals)
        scores = totals / lengths.astype(f32)[None, :]
        return preconditioned[None], jnp.roll(scores, arch, axis=0)

    return per_device


def solution(mesh):
    n_grp, n_tile, n_arch = mesh.shape["grp"], mesh.shape["tile"], mesh.shape["arch"]
    return jax.shard_map(
        make(n_grp, n_tile, n_arch),
        mesh=mesh,
        in_specs=(
            P("arch", "tile", "grp"),
            P(None, "grp"),
            P(None, "tile"),
            P("tile", "grp"),
            P("arch", "grp"),
            P("arch", "tile"),
            P("arch", None),
        ),
        out_specs=(P("arch", "grp", "tile"), P(None, "arch")),
        check_vma=False,
    )
```
